256 devices in a mesh: level: 4 (over z_hi, core), dom: 64 (over z_lo, x, y).
Axes of the slice: x: 4, y: 4, z: 8 (z_hi: 2, z_lo: 4; z = z_hi * 4 + z_lo), core: 2. Of those that a mesh axis runs over, the one named last changes fastest.
Arguments:
- loads: float32 [4, 64, 131072], P('level', None, 'dom'), may hold values from -6 to 6
- level_blocks: bfloat16 [4, 1024, 12, 128, 128], P('level', 'dom'), may hold values from -0.15625 to 0.15625
- level_cols: int32 [4, 1024, 12], P('level', 'dom'), may hold values from 0 to 27, as said below
- smoother: bfloat16 [4, 1024, 128, 128], P('level', 'dom'), may hold values from -0.375 to 0.375
- transfer_blocks: bfloat16 [4, 1024, 8, 128, 128], P('level', 'dom'), may hold values from -0.1875 to 0.1875
- transfer_cols: int32 [4, 1024, 8], P('level', 'dom'), may hold values from 0 to 15
- bound_rows: int32 [4, 64, 3, 4], P('level', 'dom'), may hold values from 0 to 15, as said below
Outputs:
- final_state: float32 [4, 64, 131072], P('level', None, 'dom')
The draws below stay inside these ranges and needn't reach their ends.
Inputs may be any that keep to these rules, and one draw needn't show every extreme that they name: `level_cols`: values below 16 name a device's own block rows; 16 + side * 4 + j names entry j of bound_rows[g, d, side]. On sections 2 and 3 a block row below 8 names only own block rows below 8 and entries j < 2; any other block row there names only own block rows from 8 on and entries j >= 2. Each list bound_rows[g, d, side] holds 4 distinct block rows of the device on that side; its first 2 entries lie below 8, the others at or above 8.
All inputs are finite; a program needn't handle non-finite values.
Results may differ from the reference program's by a relative error of at most 0.007.
Values may be sent and summed in bfloat16 or wider, within the bound.
A program may use at most 64 MiB of HBM per device.

```python
import jax
import jax.numpy as jnp
from jax import lax

BS = 128
NCOL = 64
K = 12
KT = 8
HB = 4
ITERS = 2
C1 = 8
C2 = 8
S = 16
SLABS = 64
ROWS = 131072


def pick_distinct(seed_key, lead_shape, slot_count, pick_count):
    scores = jax.random.randint(seed_key, lead_shape + (slot_count,), 0, 1 << 20)
    distinct = scores * slot_count + jnp.arange(slot_count, dtype=jnp.int32)
    return lax.top_k(distinct, pick_count)[1].astype(jnp.int32)


def draw_bound_rows(key, part):
    half_width = HB // 2
    lower_rows = pick_distinct(jax.random.fold_in(key, 11), (4, SLABS, 3), C1, half_width)
    upper_rows = pick_distinct(jax.random.fold_in(key, 12), (4, SLABS, 3), C2, half_width) + C1
    return jnp.concatenate([lower_rows, upper_rows], axis=-1).astype(jnp.int32)


def draw_level_cols(key, part):
    half_width = HB // 2
    total_rows = 4 * SLABS * S
    row_index = jnp.arange(total_rows, dtype=jnp.int32)
    section = (row_index // (SLABS * S))[:, None]
    slot_index = (row_index % S)[:, None]
    raw_draw = jax.random.randint(jax.random.fold_in(key, 21), (total_rows, K), 0, 1 << 24)
    fine_pick = raw_draw % (S + 3 * HB)
    is_first = slot_index < C1
    own_count = jnp.where(is_first, C1, C2)
    coarse_pick = raw_draw % (own_count + 3 * half_width)
    beyond = coarse_pick - own_count
    side_index = beyond // half_width
    entry_index = beyond % half_width + jnp.where(is_first, 0, half_width)
    own_col = coarse_pick + jnp.where(is_first, 0, C1)
    listed_col = S + side_index * HB + entry_index
    coarse_col = jnp.where(coarse_pick < own_count, own_col, listed_col)
    columns = jnp.where(section < 2, fine_pick, coarse_col)
    return columns.reshape(4, SLABS * S, K).astype(jnp.int32)


def set_ends(values, own_key, smallest, largest):
    longest = values.shape.index(max(values.shape))
    spots = []
    for shift in (0, 1):
        where = [jax.random.randint(jax.random.fold_in(own_key, axis), (), 0, length) for axis, length in enumerate(values.shape)]
        where[longest] = (where[longest] + shift) % values.shape[longest]
        spots.append(tuple(where))
    return values.at[spots[0]].set(smallest).at[spots[1]].set(largest)


def level_of(key, dims, shards, least, largest):
    loudness, own = 1.0, jax.random.fold_in(key, 6)
    for axis_at, shards_of in shards:
        heights = jnp.exp(jax.random.uniform(jax.random.fold_in(own, axis_at), (shards_of,), jnp.float32, least / len(shards), largest / len(shards)))
        loudness = loudness * jnp.repeat(heights, dims[axis_at] // shards_of).reshape([-1 if axis == axis_at else 1 for axis in range(len(dims))])
    return loudness


def scatter_about(own_key, shape, deviation, limit, split=(), kind=jnp.bfloat16):
    values = jax.random.normal(own_key, shape, jnp.float32) * deviation
    if len(split) > 0:
        values = level_of(own_key, shape, split, -0.22, 0.18) * values
    return jnp.clip(values, min=-limit, max=limit).astype(kind)


def setup_inputs(seed: int = 0) -> dict:
    splits = jax.random.split(jax.random.key(seed), 8)
    return {
        "loads": scatter_about(splits[0], (4, NCOL, ROWS), 1.0, 6.0, ((0, 4), (2, 64)), jnp.float32),
        "level_blocks": scatter_about(splits[1], (4, SLABS * S, K, BS, BS), (K * BS) ** -0.5, 0.15625, ((0, 4), (1, 64))),
        "level_cols": draw_level_cols(jax.random.fold_in(splits[7], 71), 0),
        "smoother": scatter_about(splits[3], (4, SLABS * S, BS, BS), (2 * BS) ** -0.5, 0.375, ((0, 4), (1, 64))),
        "transfer_blocks": scatter_about(splits[4], (4, SLABS * S, KT, BS, BS), (KT * BS) ** -0.5, 0.1875, ((0, 4), (1, 64))),
        "transfer_cols": set_ends(jax.random.randint(splits[5], (4, SLABS * S, KT), 0, S), jax.random.fold_in(splits[5], 1), 0, S - 1).astype(jnp.int32),
        "bound_rows": draw_bound_rows(jax.random.fold_in(splits[7], 71), 0),
    }


def as_panels(vector):
    return vector.reshape(4, NCOL, SLABS, S, BS)


def gather_rows(source, bound_lists):
    index_rows = bound_lists[:, None, :, :, None]
    return jnp.take_along_axis(source, index_rows, axis=3)


def extend(panels, bound_rows):
    left_side = jnp.roll(panels, 1, axis=2)
    right_side = jnp.roll(panels, -1, axis=2)
    sibling = panels[jnp.array([1, 0, 3, 2])]
    return jnp.concatenate(
        [panels,
         gather_rows(left_side, bound_rows[:, :, 0]),
         gather_rows(right_side, bound_rows[:, :, 1]),
         gather_rows(sibling, bound_rows[:, :, 2])],
        axis=3)


def apply_blocks(panels, columns, blocks, groups, per_row):
    width_ext = panels.shape[3]
    flat_panels = jnp.moveaxis(panels, 1, 2).reshape(groups * SLABS, NCOL, width_ext, BS)
    flat_columns = columns.reshape(groups * SLABS, S * per_row)
    flat_blocks = blocks.reshape(groups * SLABS, S, per_row, BS, BS)

    def one_device(operands):
        panel_set, column_set, block_set = operands
        picked = jnp.take(panel_set, column_set, axis=1).reshape(NCOL, S, per_row, BS).astype(jnp.float32)
        return jnp.einsum("cskb,skab->csa", picked, block_set.astype(jnp.float32))

    result = lax.map(one_device, (flat_panels, flat_columns, flat_blocks))
    return jnp.moveaxis(result.reshape(groups, SLABS, NCOL, S, BS), 2, 1)


def smooth(panels, smoother):
    blocks = smoother.reshape(4, SLABS, S, BS, BS).astype(jnp.float32)
    return jnp.einsum("gcdsb,gdsab->gcdsa", panels.astype(jnp.float32), blocks)


def reference(loads, level_blocks, level_cols, smoother, transfer_blocks, transfer_cols, bound_rows):
    load_panels = as_panels(loads)
    fine_loads = load_panels[0:2]
    coarse_loads = load_panels[2:4]
    iterate = jnp.zeros_like(fine_loads)
    residual = fine_loads
    blank_part = jnp.zeros(coarse_loads.shape, jnp.bfloat16)
    correction = jnp.zeros_like(load_panels)
    for cycle_index in range(ITERS):
        if cycle_index > 0:
            rounded = jnp.concatenate([iterate.astype(jnp.bfloat16), blank_part], axis=0)
            product = apply_blocks(extend(rounded, bound_rows), level_cols, level_blocks, 4, K)
            residual = fine_loads - product[0:2]
        residual_b = residual.astype(jnp.bfloat16)
        restricted = coarse_loads + apply_blocks(residual_b, transfer_cols[2:4], transfer_blocks[2:4], 2, KT)
        current = jnp.concatenate([residual, restricted], axis=0)
        first_step = smooth(current.astype(jnp.bfloat16), smoother).astype(jnp.bfloat16)
        applied = apply_blocks(extend(first_step, bound_rows), level_cols, level_blocks, 4, K)
        second_in = (current - applied).astype(jnp.bfloat16)
        correction = first_step.astype(jnp.float32) + smooth(second_in, smoother)
        coarse_b = correction[2:4].astype(jnp.bfloat16)
        iterate = iterate + correction[0:2] + apply_blocks(coarse_b, transfer_cols[0:2], transfer_blocks[0:2], 2, KT)
    final_state = jnp.concatenate([iterate, correction[2:4]], axis=0)
    return final_state.reshape(4, NCOL, SLABS * S * BS)
```

```python
import functools

import jax
import jax.numpy as jnp
from jax import lax
from jax.experimental import pallas as pl
from jax.experimental.pallas import tpu as pltpu
from jax.sharding import PartitionSpec as P

S = 16
BS = 128
K = 12
KT = 8
HB = 4
NCOL = 64
C = 2
M = NCOL // C
U = 4
PIECE = 4
NP = S // PIECE
EXT = S + 3 * HB

BF = jnp.bfloat16
F32 = jnp.float32


def dot(a, b):
    return lax.dot_general(a, b, (((1,), (0,)), ((), ())), preferred_element_type=F32)


def gathered(ref, cols_ref, i, count):
    return jnp.concatenate([ref[cols_ref[0, i, k]] for k in range(count)], axis=1)


def over_rows(body, step=U):
    def group(j, carry):
        for u in range(step):
            body(j * step + u)
        return carry

    lax.fori_loop(0, S // step, group, 0)


def panel_at(i):
    return pl.ds(pl.multiple_of(i * BS, BS), BS)


def kernel(
    loads, level, level_cols, smoother, transfer, transfer_cols, bounds, out,
    level_raw, transfer_raw, smoother_raw, level_t, transfer_t, smoother_t,
    lists, wants,
    load_sem, level_sem, transfer_sem, smoother_sem, list_sem,
    list_send, list_recv, pair_send, pair_recv, ext_send, ext_recv,
    *refs,
):
    refs = list(refs)

    def take(*dims):
        if not dims:
            return refs.pop(0)
        return [take(*dims[1:]) for _ in range(dims[0])]

    load_v = take(C)
    current = take(C)
    corr = take(C)
    state = take(C)
    outgoing = take(2, C)
    arrived = take(2, C)
    own = take(3, C)
    ext = take(3, C)
    pack = take(3, C)

    lv = lax.axis_index("level")
    dm = lax.axis_index("dom")
    doms = lax.axis_size("dom")
    fine = lv < 2
    coarse = lv >= 2
    pair = (lax.rem(lv + 2, 4), dm)
    left = (lv, lax.rem(dm + doms - 1, doms))
    right = (lv, lax.rem(dm + 1, doms))
    sibling = (lv + 1 - 2 * lax.rem(lv, 2), dm)
    mesh_ids = pl.DeviceIdType.MESH

    def load_copy(q):
        return pltpu.make_async_copy(loads.at[0, pl.ds(q * M, M)], load_v[q], load_sem.at[q])

    def level_copy(p):
        rows = pl.ds(p * PIECE, PIECE)
        return pltpu.make_async_copy(level.at[0, rows], level_raw.at[rows], level_sem.at[p])

    def transfer_copy(p):
        rows = pl.ds(p * PIECE, PIECE)
        return pltpu.make_async_copy(transfer.at[0, rows], transfer_raw.at[rows], transfer_sem.at[p])

    smoother_copy = pltpu.make_async_copy(smoother.at[0], smoother_raw, smoother_sem)
    list_copy = pltpu.make_async_copy(bounds.at[0, 0], lists, list_sem)

    def list_out(side):
        target, slot = ((left, 1), (right, 0), (sibling, 2))[side]
        return pltpu.make_async_remote_copy(
            src_ref=lists, dst_ref=wants.at[slot], send_sem=list_send.at[side],
            recv_sem=list_recv.at[slot], device_id=target, device_id_type=mesh_ids)

    def pair_out(t, q):
        return pltpu.make_async_remote_copy(
            src_ref=outgoing[t][q], dst_ref=arrived[t][q], send_sem=pair_send.at[t, q],
            recv_sem=pair_recv.at[t, q], device_id=pair, device_id_type=mesh_ids)

    def ext_out(p, q, side):
        target, slot = ((left, 1), (right, 0), (sibling, 2))[side]
        return pltpu.make_async_remote_copy(
            src_ref=pack[p][q].at[side], dst_ref=ext[p][q].at[pl.ds(S + slot * HB, HB)],
            send_sem=ext_send.at[p, q, side], recv_sem=ext_recv.at[p, q, slot],
            device_id=target, device_id_type=mesh_ids)

    def ext_in(p, q, slot):
        return ext_out(p, q, (1, 0, 2)[slot])

    def exchange(p, q):
        for side in (0, 1, 2):
            entry = (1, 0, 2)[side]
            for j in range(HB):
                pack[p][q][side, j] = own[p][q][wants[side, entry, j]]
            ext_out(p, q, side).start()

    def exchange_wait(p, q):
        for slot in range(3):
            ext_in(p, q, slot).wait_recv()

    def transpose_level():
        for p in range(NP):
            level_copy(p).wait()

            def body(j, carry):
                i = p * PIECE + j
                for k in range(K):
                    level_t[i, k * BS : (k + 1) * BS] = level_raw[i, k].T
                return carry

            lax.fori_loop(0, PIECE, body, 0)

    def transpose_transfer():
        for p in range(NP):
            transfer_copy(p).wait()

            def body(j, carry):
                i = p * PIECE + j
                for k in range(KT):
                    transfer_t[i, k * BS : (k + 1) * BS] = transfer_raw[i, k].T
                return carry

            lax.fori_loop(0, PIECE, body, 0)

    def transpose_smoother():
        smoother_copy.wait()

        def body(i, carry):
            smoother_t[i] = smoother_raw[i].T
            return carry

        lax.fori_loop(0, S, body, 0)

    def keep_step(p, q, i, first):
        own[p][q][i] = first
        ext[p][q][i] = first

    def smooth_rows(p, q, source):
        def body(i):
            keep_step(p, q, i, dot(source[i], smoother_t[i]).astype(BF))

        over_rows(body)

    def restrict_rows(t, p, q):
        def body(i):
            v = load_v[q][:, panel_at(i)] + dot(
                gathered(arrived[t][q], transfer_cols, i, KT), transfer_t[i])
            current[q][i] = v
            keep_step(p, q, i, dot(v.astype(BF), smoother_t[i]).astype(BF))

        over_rows(body)

    def second_step(p, q, give):
        def body(i):
            applied = dot(gathered(ext[p][q], level_cols, i, K), level_t[i])
            second_in = (current[q][i] - applied).astype(BF)
            give(i, own[p][q][i].astype(F32) + dot(second_in, smoother_t[i]))

        over_rows(body)

    def put(q, i, value):
        out[0, q * M : (q + 1) * M, panel_at(i)] = value

    barrier = pltpu.get_barrier_semaphore()
    for target in (left, right, sibling, pair):
        pl.semaphore_signal(barrier, inc=1, device_id=target, device_id_type=mesh_ids)

    list_copy.start()
    for q in range(C):
        load_copy(q).start()
    smoother_copy.start()

    @pl.when(fine)
    def _():
        for p in range(NP):
            level_copy(p).start()
        for p in range(NP):
            transfer_copy(p).start()
        for q in range(C):
            load_copy(q).wait()

            def body(i):
                v = load_v[q][:, panel_at(i)]
                current[q][i] = v
                outgoing[0][q][i] = v.astype(BF)

            over_rows(body)

    @pl.when(coarse)
    def _():
        for p in range(NP):
            transfer_copy(p).start()
        for p in range(NP):
            level_copy(p).start()
        for q in range(C):
            load_copy(q).wait()
        transpose_transfer()

    list_copy.wait()
    pl.semaphore_wait(barrier, 4)

    @pl.when(fine)
    def _():
        for q in range(C):
            pair_out(0, q).start()

    for side in range(3):
        list_out(side).start()
    transpose_smoother()
    for side in range(3):
        list_out((1, 0, 2)[side]).wait_recv()

    @pl.when(fine)
    def _():
        for q in range(C):
            smooth_rows(0, q, outgoing[0][q])
            exchange(0, q)
        transpose_level()
        for q in range(C):
            exchange_wait(0, q)

            def give(i, e):
                corr[q][i] = e

            second_step(0, q, give)
        transpose_transfer()
        for q in range(C):
            pair_out(0, q).wait_recv()

            def body(i):
                x = corr[q][i] + dot(gathered(arrived[0][q], transfer_cols, i, KT), transfer_t[i])
                state[q][i] = x
                keep_step(1, q, i, x.astype(BF))

            over_rows(body)
            exchange(1, q)
        for q in range(C):
            exchange_wait(1, q)

            def body(i):
                r = load_v[q][:, panel_at(i)] - dot(gathered(ext[1][q], level_cols, i, K), level_t[i])
                current[q][i] = r
                outgoing[1][q][i] = r.astype(BF)

            over_rows(body)
            pair_out(1, q).start()
            smooth_rows(2, q, outgoing[1][q])
            exchange(2, q)
        for q in range(C):
            exchange_wait(2, q)

            def give(i, e):
                state[q][i] = state[q][i] + e

            second_step(2, q, give)
        for q in range(C):
            pair_out(1, q).wait_recv()

            def body(i):
                put(q, i, state[q][i] + dot(
                    gathered(arrived[1][q], transfer_cols, i, KT), transfer_t[i]))

            over_rows(body)
        for q in range(C):
            for side in range(3):
                ext_out(2, q, side).wait_send()

    @pl.when(coarse)
    def _():
        transpose_level()
        for t in range(2):
            for q in range(C):
                pair_out(t, q).wait_recv()
                restrict_rows(t, t, q)
                exchange(t, q)
            for q in range(C):
                exchange_wait(t, q)

                def give(i, e):
                    outgoing[t][q][i] = e.astype(BF)
                    if t == 1:
                        put(q, i, e)

                second_step(t, q, give)
                pair_out(t, q).start()

    for side in range(3):
        list_out(side).wait_send()
    for t in range(2):
        for q in range(C):
            pair_out(t, q).wait_send()
            for side in range(3):
                ext_out(t, q, side).wait_send()


def local(loads, level_blocks, level_cols, smoother, transfer_blocks, transfer_cols, bound_rows):
    vmem = pltpu.VMEM
    dma = pltpu.SemaphoreType.DMA
    any_spec = pl.BlockSpec(memory_space=pl.ANY)
    smem_spec = pl.BlockSpec(memory_space=pltpu.SMEM)

    def panels(count, kind):
        return vmem((count, M, BS), kind)

    scratch = [
        vmem((S, K, BS, BS), BF), vmem((S, KT, BS, BS), BF), vmem((S, BS, BS), BF),
        vmem((S, K * BS, BS), BF), vmem((S, KT * BS, BS), BF), vmem((S, BS, BS), BF),
        pltpu.SMEM((3, HB), jnp.int32), pltpu.SMEM((3, 3, HB), jnp.int32),
        dma((C,)), dma((NP,)), dma((NP,)), dma, dma,
        dma((3,)), dma((3,)), dma((2, C)), dma((2, C)), dma((3, C, 3)), dma((3, C, 3)),
    ]
    scratch += [vmem((M, S * BS), F32)] * C
    scratch += [panels(S, F32)] * (3 * C)
    scratch += [panels(S, BF)] * (7 * C)
    scratch += [panels(EXT, BF)] * (3 * C)
    scratch += [vmem((3, HB, M, BS), BF)] * (3 * C)
    blocks = 2 * S * (3 * K + 2 * KT + 4)
    return pl.pallas_call(
        kernel,
        out_shape=jax.ShapeDtypeStruct(loads.shape, F32),
        in_specs=[any_spec, any_spec, smem_spec, any_spec, any_spec, smem_spec, any_spec],
        out_specs=pl.BlockSpec(memory_space=vmem),
        scratch_shapes=scratch,
        cost_estimate=pl.CostEstimate(
            flops=blocks * NCOL * BS * BS, bytes_accessed=12 << 20, transcendentals=0),
        compiler_params=pltpu.CompilerParams(
            collective_id=0, has_side_effects=True, vmem_limit_bytes=48 << 20),
    )(loads, level_blocks, level_cols, smoother, transfer_blocks, transfer_cols, bound_rows)


def solution(mesh):
    in_specs = (
        P("level", None, "dom"),
        P("level", "dom", None, None, None),
        P("level", "dom", None),
        P("level", "dom", None, None),
        P("level", "dom", None, None, None),
        P("level", "dom", None),
        P("level", "dom", None, None),
    )
    out_specs = P("level", None, "dom")
    return jax.shard_map(local, mesh=mesh, in_specs=in_specs, out_specs=out_specs, check_vma=False)
```

```python
import functools

import jax
import jax.numpy as jnp
from jax import lax
from jax.experimental import pallas as pl
from jax.experimental.pallas import tpu as pltpu
from jax.sharding import PartitionSpec as P

S = 16
BS = 128
K = 12
KT = 8
HB = 4
NCOL = 64
SIZES = (16, 16, 16, 16)
C = len(SIZES)
BEGIN = [sum(SIZES[:q]) for q in range(C)]
U = 8
PIECE = 4
NP = S // PIECE
EXT = S + 3 * HB

BF = jnp.bfloat16
F32 = jnp.float32


def dot(a, b):
    return lax.dot_general(a, b, (((1,), (0,)), ((), ())), preferred_element_type=F32)


def gathered(ref, cols_ref, i, count):
    return jnp.concatenate([ref[cols_ref(i, k)] for k in range(count)], axis=1)


def over_rows(body, step=U):
    def group(j, carry):
        for u in range(step):
            body(j * step + u)
        return carry

    lax.fori_loop(0, S // step, group, 0)


def panel_at(i):
    return pl.ds(pl.multiple_of(i * BS, BS), BS)


def kernel(
    loads, level, level_cols_in, smoother, transfer, transfer_cols_in, bounds, out,
    level_cols, transfer_cols,
    level_raw, transfer_raw, smoother_raw, level_t, transfer_t, smoother_t,
    lists, wants,
    load_sem, level_sem, transfer_sem, smoother_sem, list_sem, cols_sem, result_sem,
    list_send, list_recv, pair_send, pair_recv, ext_send, ext_recv,
    *refs,
):
    refs = list(refs)

    def level_col(i, k):
        return level_cols[k, 0, i]

    def transfer_col(i, k):
        return transfer_cols[0, k, i]

    def take(*dims):
        if not dims:
            return refs.pop(0)
        return [take(*dims[1:]) for _ in range(dims[0])]

    load_v = take(C)
    result = take(C)
    current = take(C)
    corr = take(C)
    state = take(C)
    outgoing = take(2, C)
    rounded = take(C)
    arrived = take(2, C)
    own = take(3, C)
    ext = take(3, C)
    pack = take(3, C)

    lv = lax.axis_index("level")
    dm = lax.axis_index("dom")
    doms = lax.axis_size("dom")
    fine = lv < 2
    coarse = lv >= 2
    pair = (lax.rem(lv + 2, 4), dm)
    left = (lv, lax.rem(dm + doms - 1, doms))
    right = (lv, lax.rem(dm + 1, doms))
    sibling = (lv + 1 - 2 * lax.rem(lv, 2), dm)
    mesh_ids = pl.DeviceIdType.MESH

    def load_copy(q):
        return pltpu.make_async_copy(loads.at[0, pl.ds(BEGIN[q], SIZES[q])], load_v[q], load_sem.at[q])

    def level_copy(p):
        rows = pl.ds(p * PIECE, PIECE)
        return pltpu.make_async_copy(level.at[0, rows], level_raw.at[rows], level_sem.at[p])

    def transfer_copy(p):
        rows = pl.ds(p * PIECE, PIECE)
        return pltpu.make_async_copy(transfer.at[0, rows], transfer_raw.at[rows], transfer_sem.at[p])

    smoother_copy = pltpu.make_async_copy(smoother.at[0], smoother_raw, smoother_sem)
    list_copy = pltpu.make_async_copy(bounds.at[0, :, 0], lists, list_sem)

    cols_copies = (
        pltpu.make_async_copy(level_cols_in, level_cols, cols_sem.at[0]),
        pltpu.make_async_copy(transfer_cols_in, transfer_cols, cols_sem.at[1]),
    )

    def list_out(side):
        target, slot = ((left, 1), (right, 0), (sibling, 2))[side]
        return pltpu.make_async_remote_copy(
            src_ref=lists, dst_ref=wants.at[slot], send_sem=list_send.at[side],
            recv_sem=list_recv.at[slot], device_id=target, device_id_type=mesh_ids)

    def pair_out(t, q):
        return pltpu.make_async_remote_copy(
            src_ref=outgoing[t][q], dst_ref=arrived[t][q], send_sem=pair_send.at[t, q],
            recv_sem=pair_recv.at[t, q], device_id=pair, device_id_type=mesh_ids)

    def pair_start(t, q):
        pair_out(t, q).start()

    def ext_out(p, q, side):
        target, slot = ((left, 1), (right, 0), (sibling, 2))[side]
        return pltpu.make_async_remote_copy(
            src_ref=pack[p][q].at[side], dst_ref=ext[p][q].at[pl.ds(S + slot * HB, HB)],
            send_sem=ext_send.at[p, q, side], recv_sem=ext_recv.at[p, q, slot],
            device_id=target, device_id_type=mesh_ids)

    def ext_in(p, q, slot):
        return ext_out(p, q, (1, 0, 2)[slot])

    def exchange(p, q):
        for side in (0, 1, 2):
            entry = (1, 0, 2)[side]
            for j in range(HB):
                pack[p][q][side, j] = own[p][q][wants[side, entry, j]]
            ext_out(p, q, side).start()

    def exchange_wait(p, q):
        for slot in range(3):
            ext_in(p, q, slot).wait_recv()

    def transpose_level():
        for p in range(NP):
            level_copy(p).wait()

            def body(j, carry):
                i = p * PIECE + j
                for k in range(K):
                    level_t[i, k * BS : (k + 1) * BS] = level_raw[i, k].T
                return carry

            lax.fori_loop(0, PIECE, body, 0)

    def transpose_transfer():
        for p in range(NP):
            transfer_copy(p).wait()

            def body(j, carry):
                i = p * PIECE + j
                for k in range(KT):
                    transfer_t[i, k * BS : (k + 1) * BS] = transfer_raw[i, k].T
                return carry

            lax.fori_loop(0, PIECE, body, 0)

    def transpose_smoother():
        smoother_copy.wait()

        def body(i, carry):
            smoother_t[i] = smoother_raw[i].T
            return carry

        lax.fori_loop(0, S, body, 0)

    def keep_step(p, q, i, first):
        own[p][q][i] = first
        ext[p][q][i] = first

    def smooth_rows(p, q, source):
        def body(i):
            keep_step(p, q, i, dot(source[i], smoother_t[i]).astype(BF))

        over_rows(body)

    def restrict_rows(t, p, q):
        def body(i):
            v = load_v[q][:, panel_at(i)] + dot(
                gathered(arrived[t][q], transfer_col, i, KT), transfer_t[i])
            current[q][i] = v
            rounded[q][i] = v.astype(BF)

        over_rows(body)
        smooth_rows(p, q, rounded[q])

    def second_step(p, q, give):
        def body(i):
            applied = dot(gathered(ext[p][q], level_col, i, K), level_t[i])
            rounded[q][i] = (current[q][i] - applied).astype(BF)

        over_rows(body)

        def finish(i):
            give(i, own[p][q][i].astype(F32) + dot(rounded[q][i], smoother_t[i]))

        over_rows(finish)

    def put(q, i, value):
        result[q][:, panel_at(i)] = value

    def result_copy(q):
        return pltpu.make_async_copy(
            result[q], out.at[0, pl.ds(BEGIN[q], SIZES[q])], result_sem.at[q])

    barrier = pltpu.get_barrier_semaphore()
    for target in (left, right, sibling, pair):
        pl.semaphore_signal(barrier, inc=1, device_id=target, device_id_type=mesh_ids)

    list_copy.start()
    for copy in cols_copies:
        copy.start()
    for q in range(C):
        load_copy(q).start()
    smoother_copy.start()

    @pl.when(fine)
    def _():
        for p in range(NP):
            level_copy(p).start()
        for p in range(NP):
            transfer_copy(p).start()
        for q in range(C):
            load_copy(q).wait()

            def body(i):
                v = load_v[q][:, panel_at(i)]
                current[q][i] = v
                outgoing[0][q][i] = v.astype(BF)

            over_rows(body)

    @pl.when(coarse)
    def _():
        for p in range(NP):
            transfer_copy(p).start()
        for p in range(NP):
            level_copy(p).start()
        for q in range(C):
            load_copy(q).wait()
        transpose_transfer()

    list_copy.wait()
    for copy in cols_copies:
        copy.wait()
    pl.semaphore_wait(barrier, 4)

    for side in range(3):
        list_out(side).start()

    @pl.when(fine)
    def _():
        for q in range(C):
            pair_start(0, q)

    transpose_smoother()
    for side in range(3):
        list_out((1, 0, 2)[side]).wait_recv()

    @pl.when(fine)
    def _():
        for q in range(C):
            smooth_rows(0, q, outgoing[0][q])
            exchange(0, q)
        transpose_level()
        for q in range(C):
            exchange_wait(0, q)

            def give(i, e):
                corr[q][i] = e

            second_step(0, q, give)
        transpose_transfer()
        for q in range(C):
            pair_out(0, q).wait_recv()

            def body(i):
                x = corr[q][i] + dot(gathered(arrived[0][q], transfer_col, i, KT), transfer_t[i])
                state[q][i] = x
                keep_step(1, q, i, x.astype(BF))

            over_rows(body)
            exchange(1, q)
        for q in range(C):
            exchange_wait(1, q)

            def body(i):
                r = load_v[q][:, panel_at(i)] - dot(gathered(ext[1][q], level_col, i, K), level_t[i])
                current[q][i] = r
                outgoing[1][q][i] = r.astype(BF)

            over_rows(body)
            pair_start(1, q)
        for q in range(C):
            smooth_rows(2, q, outgoing[1][q])
            exchange(2, q)
        for q in range(C):
            exchange_wait(2, q)

            def give(i, e):
                state[q][i] = state[q][i] + e

            second_step(2, q, give)
        for q in range(C):
            pair_out(1, q).wait_recv()

            def body(i):
                put(q, i, state[q][i] + dot(
                    gathered(arrived[1][q], transfer_col, i, KT), transfer_t[i]))

            over_rows(body)
            result_copy(q).start()
        for q in range(C):
            for side in range(3):
                ext_out(2, q, side).wait_send()

    @pl.when(coarse)
    def _():
        transpose_level()
        for t in range(2):
            for q in range(C):
                pair_out(t, q).wait_recv()
                restrict_rows(t, t, q)
                exchange(t, q)
            for q in range(C):
                exchange_wait(t, q)

                def give(i, e):
                    outgoing[t][q][i] = e.astype(BF)
                    if t == 1:
                        put(q, i, e)

                second_step(t, q, give)
                pair_start(t, q)
                if t == 1:
                    result_copy(q).start()

    for q in range(C):
        result_copy(q).wait()
    for side in range(3):
        list_out(side).wait_send()
    for t in range(2):
        for q in range(C):
            pair_out(t, q).wait_send()
            for side in range(3):
                ext_out(t, q, side).wait_send()


def local(loads, level_blocks, level_cols, smoother, transfer_blocks, transfer_cols, bound_rows):
    vmem = pltpu.VMEM
    dma = pltpu.SemaphoreType.DMA
    any_spec = pl.BlockSpec(memory_space=pltpu.HBM)

    def each(kind, *dims):
        return [vmem(tuple(m if n is None else n for n in dims), kind) for m in SIZES]

    scratch = [
        pltpu.SMEM((K, 1, S), jnp.int32), pltpu.SMEM((1, KT, S), jnp.int32),
        vmem((S, K, BS, BS), BF), vmem((S, KT, BS, BS), BF), vmem((S, BS, BS), BF),
        vmem((S, K * BS, BS), BF), vmem((S, KT * BS, BS), BF), vmem((S, BS, BS), BF),
        pltpu.SMEM((3, HB), jnp.int32), pltpu.SMEM((3, 3, HB), jnp.int32),
        dma((C,)), dma((NP,)), dma((NP,)), dma, dma, dma((2,)), dma((C,)),
        dma((3,)), dma((3,)), dma((2, C)), dma((2, C)), dma((3, C, 3)), dma((3, C, 3)),
    ]
    scratch += each(F32, None, S * BS) * 2
    scratch += each(F32, S, None, BS) * 3
    scratch += each(BF, S, None, BS) * 8
    scratch += each(BF, EXT, None, BS) * 3
    scratch += each(BF, 3, HB, None, BS) * 3
    blocks = 2 * S * (3 * K + 2 * KT + 4)
    return pl.pallas_call(
        kernel,
        out_shape=jax.ShapeDtypeStruct(loads.shape, F32),
        in_specs=[any_spec] * 7,
        out_specs=any_spec,
        scratch_shapes=scratch,
        cost_estimate=pl.CostEstimate(
            flops=blocks * NCOL * BS * BS, bytes_accessed=12 << 20, transcendentals=0),
        compiler_params=pltpu.CompilerParams(
            collective_id=0, has_side_effects=True, vmem_limit_bytes=64 << 20),
    )(
        loads, level_blocks, jnp.transpose(level_cols, (2, 0, 1)), smoother, transfer_blocks,
        jnp.transpose(transfer_cols, (0, 2, 1)), jnp.transpose(bound_rows, (0, 2, 1, 3)))


def solution(mesh):
    in_specs = (
        P("level", None, "dom"),
        P("level", "dom", None, None, None),
        P("level", "dom", None),
        P("level", "dom", None, None),
        P("level", "dom", None, None, None),
        P("level", "dom", None),
        P("level", "dom", None, None),
    )
    out_specs = P("level", None, "dom")
    return jax.shard_map(local, mesh=mesh, in_specs=in_specs, out_specs=out_specs, check_vma=False)
```

```python
import functools

import jax
import jax.numpy as jnp
from jax import lax
from jax.experimental import pallas as pl
from jax.experimental.pallas import tpu as pltpu
from jax.sharding import PartitionSpec as P

S = 16
BS = 128
K = 12
KT = 8
HB = 4
NCOL = 64
SIZES = (16, 16, 16, 16)
C = len(SIZES)
BEGIN = [sum(SIZES[:q]) for q in range(C)]
U = 8
PIECE = 4
NP = S // PIECE
EXT = S + 3 * HB

BF = jnp.bfloat16
F32 = jnp.float32


def dot(a, b):
    return lax.dot_general(a, b, (((1,), (0,)), ((), ())), preferred_element_type=F32)


def gathered(ref, cols_ref, i, count):
    return jnp.concatenate([ref[cols_ref(i, k)] for k in range(count)], axis=1)


def over_rows(body, step=U):
    def group(j, carry):
        for u in range(step):
            body(j * step + u)
        return carry

    lax.fori_loop(0, S // step, group, 0)


def panel_at(i):
    return pl.ds(pl.multiple_of(i * BS, BS), BS)


def kernel(
    loads, level, level_cols_in, smoother, transfer, transfer_cols_in, bounds, out,
    level_cols, transfer_cols,
    level_raw, transfer_raw, smoother_raw, level_t, transfer_t, smoother_t,
    lists, wants,
    load_sem, level_sem, transfer_sem, smoother_sem, list_sem, cols_sem, result_sem,
    list_send, list_recv, pair_send, pair_recv, ext_send, ext_recv,
    *refs,
):
    refs = list(refs)

    def level_col(i, k):
        return level_cols[k, 0, i]

    def transfer_col(i, k):
        return transfer_cols[0, k, i]

    def take(*dims):
        if not dims:
            return refs.pop(0)
        return [take(*dims[1:]) for _ in range(dims[0])]

    load_v = take(C)
    result = take(C)
    current = take(C)
    corr = take(C)
    state = take(C)
    outgoing = take(2, C)
    rounded = take(C)
    arrived = take(2, C)
    own = take(3, C)
    ext = take(3, C)
    pack = take(3, C)

    lv = lax.axis_index("level")
    dm = lax.axis_index("dom")
    doms = lax.axis_size("dom")
    fine = lv < 2
    coarse = lv >= 2
    pair = (lax.rem(lv + 2, 4), dm)
    left = (lv, lax.rem(dm + doms - 1, doms))
    right = (lv, lax.rem(dm + 1, doms))
    sibling = (lv + 1 - 2 * lax.rem(lv, 2), dm)
    mesh_ids = pl.DeviceIdType.MESH

    def load_copy(q):
        return pltpu.make_async_copy(loads.at[0, pl.ds(BEGIN[q], SIZES[q])], load_v[q], load_sem.at[q])

    def level_copy(p):
        rows = pl.ds(p * PIECE, PIECE)
        return pltpu.make_async_copy(level.at[0, rows], level_raw.at[rows], level_sem.at[p])

    def transfer_copy(p):
        rows = pl.ds(p * PIECE, PIECE)
        return pltpu.make_async_copy(transfer.at[0, rows], transfer_raw.at[rows], transfer_sem.at[p])

    smoother_copy = pltpu.make_async_copy(smoother.at[0], smoother_raw, smoother_sem)
    list_copy = pltpu.make_async_copy(bounds.at[0, :, 0], lists, list_sem)

    cols_copies = (
        pltpu.make_async_copy(level_cols_in, level_cols, cols_sem.at[0]),
        pltpu.make_async_copy(transfer_cols_in, transfer_cols, cols_sem.at[1]),
    )

    def list_out(side):
        target, slot = ((left, 1), (right, 0), (sibling, 2))[side]
        return pltpu.make_async_remote_copy(
            src_ref=lists, dst_ref=wants.at[slot], send_sem=list_send.at[side],
            recv_sem=list_recv.at[slot], device_id=target, device_id_type=mesh_ids)

    def pair_out(t, q):
        return pltpu.make_async_remote_copy(
            src_ref=outgoing[t][q], dst_ref=arrived[t][q], send_sem=pair_send.at[t, q],
            recv_sem=pair_recv.at[t, q], device_id=pair, device_id_type=mesh_ids)

    def pair_start(t, q):
        pair_out(t, q).start()

    def ext_out(p, q, side):
        target, slot = ((left, 1), (right, 0), (sibling, 2))[side]
        return pltpu.make_async_remote_copy(
            src_ref=pack[p][q].at[side], dst_ref=ext[p][q].at[pl.ds(S + slot * HB, HB)],
            send_sem=ext_send.at[p, q, side], recv_sem=ext_recv.at[p, q, slot],
            device_id=target, device_id_type=mesh_ids)

    def ext_in(p, q, slot):
        return ext_out(p, q, (1, 0, 2)[slot])

    def exchange(p, q):
        for side in (0, 1, 2):
            entry = (1, 0, 2)[side]
            for j in range(HB):
                pack[p][q][side, j] = own[p][q][wants[side, entry, j]]
            ext_out(p, q, side).start()

    def exchange_wait(p, q):
        for slot in range(3):
            ext_in(p, q, slot).wait_recv()

    def transpose_level():
        for p in range(NP):
            level_copy(p).wait()

            def body(j, carry):
                i = p * PIECE + j
                for k in range(K):
                    level_t[i, k * BS : (k + 1) * BS] = level_raw[i, k].T
                return carry

            lax.fori_loop(0, PIECE, body, 0)

    def transpose_transfer():
        for p in range(NP):
            transfer_copy(p).wait()

            def body(j, carry):
                i = p * PIECE + j
                for k in range(KT):
                    transfer_t[i, k * BS : (k + 1) * BS] = transfer_raw[i, k].T
                return carry

            lax.fori_loop(0, PIECE, body, 0)

    def transpose_smoother():
        smoother_copy.wait()

        def body(i):
            smoother_t[i] = smoother_raw[i].T

        over_rows(body)

    def keep_step(p, q, i, first):
        own[p][q][i] = first
        ext[p][q][i] = first

    def smooth_rows(p, q, source):
        def body(i):
            keep_step(p, q, i, dot(source[i], smoother_t[i]).astype(BF))

        over_rows(body)

    def restrict_rows(t, p, q):
        def body(i):
            v = load_v[q][:, panel_at(i)] + dot(
                gathered(arrived[t][q], transfer_col, i, KT), transfer_t[i])
            current[q][i] = v
            rounded[q][i] = v.astype(BF)

        over_rows(body)
        smooth_rows(p, q, rounded[q])

    def second_step(p, q, give):
        def body(i):
            applied = dot(gathered(ext[p][q], level_col, i, K), level_t[i])
            rounded[q][i] = (current[q][i] - applied).astype(BF)

        over_rows(body)

        def finish(i):
            give(i, own[p][q][i].astype(F32) + dot(rounded[q][i], smoother_t[i]))

        over_rows(finish)

    def put(q, i, value):
        result[q][:, panel_at(i)] = value

    def result_copy(q):
        return pltpu.make_async_copy(
            result[q], out.at[0, pl.ds(BEGIN[q], SIZES[q])], result_sem.at[q])

    barrier = pltpu.get_barrier_semaphore()
    for target in (left, right, sibling, pair):
        pl.semaphore_signal(barrier, inc=1, device_id=target, device_id_type=mesh_ids)

    list_copy.start()
    for copy in cols_copies:
        copy.start()
    for q in range(C):
        load_copy(q).start()
    smoother_copy.start()

    @pl.when(fine)
    def _():
        for p in range(NP):
            level_copy(p).start()
        for p in range(NP):
            transfer_copy(p).start()
        for q in range(C):
            load_copy(q).wait()

            def body(i):
                v = load_v[q][:, panel_at(i)]
                current[q][i] = v
                outgoing[0][q][i] = v.astype(BF)

            over_rows(body)

    @pl.when(coarse)
    def _():
        for p in range(NP):
            transfer_copy(p).start()
        for p in range(NP):
            level_copy(p).start()
        for q in range(C):
            load_copy(q).wait()
        transpose_transfer()

    list_copy.wait()
    for copy in cols_copies:
        copy.wait()
    pl.semaphore_wait(barrier, 4)

    for side in range(3):
        list_out(side).start()

    @pl.when(fine)
    def _():
        for q in range(C):
            pair_start(0, q)

    transpose_smoother()
    transpose_level()

    def lists_wait():
        for side in range(3):
            list_out((1, 0, 2)[side]).wait_recv()

    @pl.when(fine)
    def _():
        lists_wait()
        for q in range(C):
            smooth_rows(0, q, outgoing[0][q])
            exchange(0, q)
        for q in range(C):
            exchange_wait(0, q)

            def give(i, e):
                corr[q][i] = e

            second_step(0, q, give)
        transpose_transfer()
        for q in range(C):
            pair_out(0, q).wait_recv()

            def body(i):
                x = corr[q][i] + dot(gathered(arrived[0][q], transfer_col, i, KT), transfer_t[i])
                state[q][i] = x
                keep_step(1, q, i, x.astype(BF))

            over_rows(body)
            exchange(1, q)
        for q in range(C):
            exchange_wait(1, q)

            def body(i):
                r = load_v[q][:, panel_at(i)] - dot(gathered(ext[1][q], level_col, i, K), level_t[i])
                current[q][i] = r
                outgoing[1][q][i] = r.astype(BF)

            over_rows(body)
            pair_start(1, q)
        for q in range(C):
            smooth_rows(2, q, outgoing[1][q])
            exchange(2, q)
        for q in range(C):
            exchange_wait(2, q)

            def give(i, e):
                state[q][i] = state[q][i] + e

            second_step(2, q, give)
        for q in range(C):
            pair_out(1, q).wait_recv()

            def body(i):
                put(q, i, state[q][i] + dot(
                    gathered(arrived[1][q], transfer_col, i, KT), transfer_t[i]))

            over_rows(body)
            result_copy(q).start()
        for q in range(C):
            for side in range(3):
                ext_out(2, q, side).wait_send()

    @pl.when(coarse)
    def _():
        for t in range(2):
            for q in range(C):
                pair_out(t, q).wait_recv()
                restrict_rows(t, t, q)
                if t == 0 and q == 0:
                    lists_wait()
                exchange(t, q)
            for q in range(C):
                exchange_wait(t, q)

                def give(i, e):
                    outgoing[t][q][i] = e.astype(BF)
                    if t == 1:
                        put(q, i, e)

                second_step(t, q, give)
                pair_start(t, q)
                if t == 1:
                    result_copy(q).start()

    for q in range(C):
        result_copy(q).wait()
    for side in range(3):
        list_out(side).wait_send()
    for t in range(2):
        for q in range(C):
            pair_out(t, q).wait_send()
            for side in range(3):
                ext_out(t, q, side).wait_send()


def local(loads, level_blocks, level_cols, smoother, transfer_blocks, transfer_cols, bound_rows):
    vmem = pltpu.VMEM
    dma = pltpu.SemaphoreType.DMA
    any_spec = pl.BlockSpec(memory_space=pltpu.HBM)

    def each(kind, *dims):
        return [vmem(tuple(m if n is None else n for n in dims), kind) for m in SIZES]

    scratch = [
        pltpu.SMEM((K, 1, S), jnp.int32), pltpu.SMEM((1, KT, S), jnp.int32),
        vmem((S, K, BS, BS), BF), vmem((S, KT, BS, BS), BF), vmem((S, BS, BS), BF),
        vmem((S, K * BS, BS), BF), vmem((S, KT * BS, BS), BF), vmem((S, BS, BS), BF),
        pltpu.SMEM((3, HB), jnp.int32), pltpu.SMEM((3, 3, HB), jnp.int32),
        dma((C,)), dma((NP,)), dma((NP,)), dma, dma, dma((2,)), dma((C,)),
        dma((3,)), dma((3,)), dma((2, C)), dma((2, C)), dma((3, C, 3)), dma((3, C, 3)),
    ]
    scratch += each(F32, None, S * BS) * 2
    scratch += each(F32, S, None, BS) * 3
    scratch += each(BF, S, None, BS) * 8
    scratch += each(BF, EXT, None, BS) * 3
    scratch += each(BF, 3, HB, None, BS) * 3
    blocks = 2 * S * (3 * K + 2 * KT + 4)
    return pl.pallas_call(
        kernel,
        out_shape=jax.ShapeDtypeStruct(loads.shape, F32),
        in_specs=[any_spec] * 7,
        out_specs=any_spec,
        scratch_shapes=scratch,
        cost_estimate=pl.CostEstimate(
            flops=blocks * NCOL * BS * BS, bytes_accessed=12 << 20, transcendentals=0),
        compiler_params=pltpu.CompilerParams(
            collective_id=0, has_side_effects=True, vmem_limit_bytes=48 << 20),
    )(*(pltpu.with_memory_space_constraint(a, pltpu.HBM) for a in (
        loads, level_blocks, jnp.transpose(level_cols, (2, 0, 1)), smoother, transfer_blocks,
        jnp.transpose(transfer_cols, (0, 2, 1)), jnp.transpose(bound_rows, (0, 2, 1, 3)))))


def solution(mesh):
    in_specs = (
        P("level", None, "dom"),
        P("level", "dom", None, None, None),
        P("level", "dom", None),
        P("level", "dom", None, None),
        P("level", "dom", None, None, None),
        P("level", "dom", None),
        P("level", "dom", None, None),
    )
    out_specs = P("level", None, "dom")
    return jax.shard_map(local, mesh=mesh, in_specs=in_specs, out_specs=out_specs, check_vma=False)
```

```python
import functools

import jax
import jax.numpy as jnp
from jax import lax
from jax.experimental import pallas as pl
from jax.experimental.pallas import tpu as pltpu
from jax.sharding import PartitionSpec as P

S = 16
BS = 128
K = 12
KT = 8
HB = 4
NCOL = 64
SIZES = (16, 16, 16, 16)
C = len(SIZES)
BEGIN = [sum(SIZES[:q]) for q in range(C)]
U = 16
PIECE = 4
NP = S // PIECE
EXT = S + 3 * HB

BF = jnp.bfloat16
F32 = jnp.float32


def dot(a, b):
    return lax.dot_general(a, b, (((1,), (0,)), ((), ())), preferred_element_type=F32)


def gathered(ref, cols_ref, i, count):
    return jnp.concatenate([ref[cols_ref(i, k)] for k in range(count)], axis=1)


def over_rows(body, step=U):
    def group(j, carry):
        for u in range(step):
            body(j * step + u)
        return carry

    lax.fori_loop(0, S // step, group, 0)


def panel_at(i):
    return pl.ds(pl.multiple_of(i * BS, BS), BS)


def kernel(
    loads, level, level_cols_in, smoother, transfer, transfer_cols_in, bounds, out,
    level_cols, transfer_cols,
    level_raw, transfer_raw, smoother_raw, level_t, transfer_t, smoother_t,
    lists, wants,
    load_sem, level_sem, transfer_sem, smoother_sem, list_sem, cols_sem, result_sem,
    list_send, list_recv, pair_send, pair_recv, ext_send, ext_recv,
    *refs,
):
    refs = list(refs)

    def level_col(i, k):
        return level_cols[k, 0, i]

    def transfer_col(i, k):
        return transfer_cols[0, k, i]

    def take(*dims):
        if not dims:
            return refs.pop(0)
        return [take(*dims[1:]) for _ in range(dims[0])]

    load_v = take(C)
    result = take(C)
    current = take(C)
    corr = take(C)
    state = take(C)
    outgoing = take(2, C)
    rounded = take(C)
    arrived = take(2, C)
    own = take(3, C)
    ext = take(3, C)
    pack = take(3, C)

    lv = lax.axis_index("level")
    dm = lax.axis_index("dom")
    doms = lax.axis_size("dom")
    fine = lv < 2
    coarse = lv >= 2
    pair = (lax.rem(lv + 2, 4), dm)
    left = (lv, lax.rem(dm + doms - 1, doms))
    right = (lv, lax.rem(dm + 1, doms))
    sibling = (lv + 1 - 2 * lax.rem(lv, 2), dm)
    mesh_ids = pl.DeviceIdType.MESH

    def load_copy(q):
        return pltpu.make_async_copy(loads.at[0, pl.ds(BEGIN[q], SIZES[q])], load_v[q], load_sem.at[q])

    def level_copy(p):
        rows = pl.ds(p * PIECE, PIECE)
        return pltpu.make_async_copy(level.at[0, rows], level_raw.at[rows], level_sem.at[p])

    def transfer_copy(p):
        rows = pl.ds(p * PIECE, PIECE)
        return pltpu.make_async_copy(transfer.at[0, rows], transfer_raw.at[rows], transfer_sem.at[p])

    smoother_copy = pltpu.make_async_copy(smoother.at[0], smoother_raw, smoother_sem)
    list_copy = pltpu.make_async_copy(bounds.at[0, :, 0], lists, list_sem)

    cols_copies = (
        pltpu.make_async_copy(level_cols_in, level_cols, cols_sem.at[0]),
        pltpu.make_async_copy(transfer_cols_in, transfer_cols, cols_sem.at[1]),
    )

    def list_out(side):
        target, slot = ((left, 1), (right, 0), (sibling, 2))[side]
        return pltpu.make_async_remote_copy(
            src_ref=lists, dst_ref=wants.at[slot], send_sem=list_send.at[side],
            recv_sem=list_recv.at[slot], device_id=target, device_id_type=mesh_ids)

    def pair_out(t, q):
        return pltpu.make_async_remote_copy(
            src_ref=outgoing[t][q], dst_ref=arrived[t][q], send_sem=pair_send.at[t, q],
            recv_sem=pair_recv.at[t, q], device_id=pair, device_id_type=mesh_ids)

    def pair_start(t, q):
        pair_out(t, q).start()

    def ext_out(p, q, side):
        target, slot = ((left, 1), (right, 0), (sibling, 2))[side]
        return pltpu.make_async_remote_copy(
            src_ref=pack[p][q].at[side], dst_ref=ext[p][q].at[pl.ds(S + slot * HB, HB)],
            send_sem=ext_send.at[p, q, side], recv_sem=ext_recv.at[p, q, slot],
            device_id=target, device_id_type=mesh_ids)

    def ext_in(p, q, slot):
        return ext_out(p, q, (1, 0, 2)[slot])

    def exchange(p, q):
        for side in (0, 1, 2):
            entry = (1, 0, 2)[side]
            for j in range(HB):
                pack[p][q][side, j] = own[p][q][wants[side, entry, j]]
            ext_out(p, q, side).start()

    def exchange_wait(p, q):
        for slot in range(3):
            ext_in(p, q, slot).wait_recv()

    def transpose_level():
        for p in range(NP):
            level_copy(p).wait()

            def body(j, carry):
                i = p * PIECE + j
                for k in range(K):
                    level_t[i, k * BS : (k + 1) * BS] = level_raw[i, k].T
                return carry

            lax.fori_loop(0, PIECE, body, 0)

    def transpose_transfer():
        for p in range(NP):
            transfer_copy(p).wait()

            def body(j, carry):
                i = p * PIECE + j
                for k in range(KT):
                    transfer_t[i, k * BS : (k + 1) * BS] = transfer_raw[i, k].T
                return carry

            lax.fori_loop(0, PIECE, body, 0)

    def transpose_smoother():
        smoother_copy.wait()

        def body(i):
            smoother_t[i] = smoother_raw[i].T

        over_rows(body)

    def keep_step(p, q, i, first):
        own[p][q][i] = first
        ext[p][q][i] = first

    def smooth_rows(p, q, source):
        def body(i):
            keep_step(p, q, i, dot(source[i], smoother_t[i]).astype(BF))

        over_rows(body)

    def restrict_rows(t, p, q):
        def body(i):
            v = load_v[q][:, panel_at(i)] + dot(
                gathered(arrived[t][q], transfer_col, i, KT), transfer_t[i])
            current[q][i] = v
            rounded[q][i] = v.astype(BF)

        over_rows(body)
        smooth_rows(p, q, rounded[q])

    def second_step(p, q, give):
        def body(i):
            applied = dot(gathered(ext[p][q], level_col, i, K), level_t[i])
            rounded[q][i] = (current[q][i] - applied).astype(BF)

        over_rows(body)

        def finish(i):
            give(i, own[p][q][i].astype(F32) + dot(rounded[q][i], smoother_t[i]))

        over_rows(finish)

    def put(q, i, value):
        result[q][:, panel_at(i)] = value

    def result_copy(q):
        return pltpu.make_async_copy(
            result[q], out.at[0, pl.ds(BEGIN[q], SIZES[q])], result_sem.at[q])

    barrier = pltpu.get_barrier_semaphore()
    for target in (left, right, sibling, pair):
        pl.semaphore_signal(barrier, inc=1, device_id=target, device_id_type=mesh_ids)

    list_copy.start()
    for copy in cols_copies:
        copy.start()
    for q in range(C):
        load_copy(q).start()
    smoother_copy.start()

    @pl.when(fine)
    def _():
        for p in range(NP):
            level_copy(p).start()
        for p in range(NP):
            transfer_copy(p).start()
        for q in range(C):
            load_copy(q).wait()

            def body(i):
                v = load_v[q][:, panel_at(i)]
                current[q][i] = v
                outgoing[0][q][i] = v.astype(BF)

            over_rows(body)

    @pl.when(coarse)
    def _():
        for p in range(NP):
            transfer_copy(p).start()
        for p in range(NP):
            level_copy(p).start()
        for q in range(C):
            load_copy(q).wait()
        transpose_transfer()

    list_copy.wait()
    for copy in cols_copies:
        copy.wait()
    pl.semaphore_wait(barrier, 4)

    for side in range(3):
        list_out(side).start()

    @pl.when(fine)
    def _():
        for q in range(C):
            pair_start(0, q)

    transpose_smoother()
    transpose_level()

    def lists_wait():
        for side in range(3):
            list_out((1, 0, 2)[side]).wait_recv()

    @pl.when(fine)
    def _():
        lists_wait()
        for q in range(C):
            smooth_rows(0, q, outgoing[0][q])
            exchange(0, q)
        for q in range(C):
            exchange_wait(0, q)

            def give(i, e):
                corr[q][i] = e

            second_step(0, q, give)
        transpose_transfer()
        for q in range(C):
            pair_out(0, q).wait_recv()

            def body(i):
                x = corr[q][i] + dot(gathered(arrived[0][q], transfer_col, i, KT), transfer_t[i])
                state[q][i] = x
                keep_step(1, q, i, x.astype(BF))

            over_rows(body)
            exchange(1, q)
        for q in range(C):
            exchange_wait(1, q)

            def body(i):
                r = load_v[q][:, panel_at(i)] - dot(gathered(ext[1][q], level_col, i, K), level_t[i])
                current[q][i] = r
                outgoing[1][q][i] = r.astype(BF)

            over_rows(body)
            pair_start(1, q)
        for q in range(C):
            smooth_rows(2, q, outgoing[1][q])
            exchange(2, q)
        for q in range(C):
            exchange_wait(2, q)

            def give(i, e):
                state[q][i] = state[q][i] + e

            second_step(2, q, give)
        for q in range(C):
            pair_out(1, q).wait_recv()

            def body(i):
                put(q, i, state[q][i] + dot(
                    gathered(arrived[1][q], transfer_col, i, KT), transfer_t[i]))

            over_rows(body)
            result_copy(q).start()
        for q in range(C):
            for side in range(3):
                ext_out(2, q, side).wait_send()

    @pl.when(coarse)
    def _():
        for t in range(2):
            for q in range(C):
                pair_out(t, q).wait_recv()
                restrict_rows(t, t, q)
                if t == 0 and q == 0:
                    lists_wait()
                exchange(t, q)
            for q in range(C):
                exchange_wait(t, q)

                def give(i, e):
                    outgoing[t][q][i] = e.astype(BF)
                    if t == 1:
                        put(q, i, e)

                second_step(t, q, give)
                pair_start(t, q)
                if t == 1:
                    result_copy(q).start()

    for q in range(C):
        result_copy(q).wait()
    for side in range(3):
        list_out(side).wait_send()
    for t in range(2):
        for q in range(C):
            pair_out(t, q).wait_send()
            for side in range(3):
                ext_out(t, q, side).wait_send()


def local(loads, level_blocks, level_cols, smoother, transfer_blocks, transfer_cols, bound_rows):
    vmem = pltpu.VMEM
    dma = pltpu.SemaphoreType.DMA
    any_spec = pl.BlockSpec(memory_space=pltpu.HBM)

    def each(kind, *dims):
        return [vmem(tuple(m if n is None else n for n in dims), kind) for m in SIZES]

    scratch = [
        pltpu.SMEM((K, 1, S), jnp.int32), pltpu.SMEM((1, KT, S), jnp.int32),
        vmem((S, K, BS, BS), BF), vmem((S, KT, BS, BS), BF), vmem((S, BS, BS), BF),
        vmem((S, K * BS, BS), BF), vmem((S, KT * BS, BS), BF), vmem((S, BS, BS), BF),
        pltpu.SMEM((3, HB), jnp.int32), pltpu.SMEM((3, 3, HB), jnp.int32),
        dma((C,)), dma((NP,)), dma((NP,)), dma, dma, dma((2,)), dma((C,)),
        dma((3,)), dma((3,)), dma((2, C)), dma((2, C)), dma((3, C, 3)), dma((3, C, 3)),
    ]
    scratch += each(F32, None, S * BS) * 2
    scratch += each(F32, S, None, BS) * 3
    scratch += each(BF, S, None, BS) * 8
    scratch += each(BF, EXT, None, BS) * 3
    scratch += each(BF, 3, HB, None, BS) * 3
    blocks = 2 * S * (3 * K + 2 * KT + 4)
    return pl.pallas_call(
        kernel,
        out_shape=jax.ShapeDtypeStruct(loads.shape, F32),
        in_specs=[any_spec] * 7,
        out_specs=any_spec,
        scratch_shapes=scratch,
        cost_estimate=pl.CostEstimate(
            flops=blocks * NCOL * BS * BS, bytes_accessed=12 << 20, transcendentals=0),
        compiler_params=pltpu.CompilerParams(
            collective_id=0, has_side_effects=True, vmem_limit_bytes=48 << 20),
    )(*(pltpu.with_memory_space_constraint(a, pltpu.HBM) for a in (
        loads, level_blocks, jnp.transpose(level_cols, (2, 0, 1)), smoother, transfer_blocks,
        jnp.transpose(transfer_cols, (0, 2, 1)), jnp.transpose(bound_rows, (0, 2, 1, 3)))))


def solution(mesh):
    in_specs = (
        P("level", None, "dom"),
        P("level", "dom", None, None, None),
        P("level", "dom", None),
        P("level", "dom", None, None),
        P("level", "dom", None, None, None),
        P("level", "dom", None),
        P("level", "dom", None, None),
    )
    out_specs = P("level", None, "dom")
    return jax.shard_map(local, mesh=mesh, in_specs=in_specs, out_specs=out_specs, check_vma=False)
```
